128 devices in a mesh: grid: 4 (over y_hi, core), tile: 32 (over y_lo, x, z).
Axes of the slice: x: 4, y: 4 (y_hi: 2, y_lo: 2; y = y_hi * 2 + y_lo), z: 4, core: 2. Of those that a mesh axis runs over, the one named last changes fastest.
Arguments:
- state_field: float32 [4, 512, 4, 4, 4, 4, 128], P('grid', 'tile'), may hold values from -6 to 6
- levels: int32 [4, 6], P('grid'), may hold values from 1 to 4
- sign_bits: int32 [4], P('grid'), may hold values from 0 to 1
Outputs:
- combined_field: float32 [4, 512, 4, 4, 4, 4, 128], P('grid', 'tile')
The draws below stay inside these ranges and needn't reach their ends.
All inputs are finite; a program needn't handle non-finite values.
Results may differ from the reference program's by a relative error of at most 0.0003.
Values sent between devices are 32-bit elements; how exact they have to be, the bound alone decides.
No kernel may reach another device: no remote copies, remote signals or barrier semaphores. Data moves between devices by JAX's collectives and lax.ppermute only.
A program may use at most 64 MiB of HBM per device.

```python
import jax
import jax.numpy as jnp
import numpy as np
from jax import lax

Q = 4
L = 128
STEPS = 4
GRIDS = 4
NX = 512


def set_ends(values, key, low, top_value):
    longest = values.shape.index(max(values.shape))
    spots = []
    for shift in (0, 1):
        where = [jax.random.randint(jax.random.fold_in(key, axis), (), 0, length) for axis, length in enumerate(values.shape)]
        where[longest] = (where[longest] + shift) % values.shape[longest]
        spots.append(tuple(where))
    return values.at[spots[0]].set(low).at[spots[1]].set(top_value)


def block_levels(key, extent, split, low, largest):
    def one(axis_at, parts):
        heights = jax.random.uniform(jax.random.fold_in(jax.random.fold_in(key, 6), axis_at), (parts,), jnp.float32, low / len(split), largest / len(split))
        return jnp.repeat(jnp.exp(heights), extent[axis_at] // parts).reshape((-1,) + (1,) * (len(extent) - axis_at - 1))

    loudness = one(*split[0])
    for cut in split[1:]:
        loudness = loudness * one(*cut)
    return loudness


def bell_draw(own_key, shape, deviation, limit, split=(), dtype=jnp.bfloat16):
    values = deviation * jax.random.normal(own_key, shape, jnp.float32)
    if split:
        values = values * block_levels(own_key, shape, split, -0.22, 0.18)
    return jnp.clip(values, -limit, limit).astype(dtype)


def setup_inputs(seed: int = 0) -> dict:
    splits = jax.random.split(jax.random.key(seed), 4)
    state_field = bell_draw(splits[0], (GRIDS, NX, Q, Q, Q, Q, L), 1.0, 6.0, ((0, 4), (1, 32)), jnp.float32)
    levels = set_ends(jax.random.randint(splits[1], (GRIDS, 6), 1, 5), jax.random.fold_in(splits[1], 1), 1, 4).astype(jnp.int32)
    sign_bits = set_ends(jax.random.randint(splits[2], (GRIDS,), 0, 2), jax.random.fold_in(splits[2], 1), 0, 1).astype(jnp.int32)
    return {"state_field": state_field, "levels": levels, "sign_bits": sign_bits}


def hierarchize(values):
    points = values.shape[0]
    stride = 1
    while stride < points:
        blocks = values.reshape(points // (2 * stride), 2 * stride, -1)
        anchor = blocks[:, 0]
        right = jnp.roll(anchor, -1, 0)
        blocks = blocks.at[:, stride].add(-0.5 * (anchor + right))
        values = blocks.reshape(points, -1)
        stride = stride * 2
    return values


def dehierarchize(values):
    points = values.shape[0]
    stride = points // 2
    while stride >= 1:
        blocks = values.reshape(points // (2 * stride), 2 * stride, -1)
        anchor = blocks[:, 0]
        right = jnp.roll(anchor, -1, 0)
        blocks = blocks.at[:, stride].add(0.5 * (anchor + right))
        values = blocks.reshape(points, -1)
        stride = stride // 2
    return values


def level_depth(points):
    depth_max = points.bit_length() - 1
    position = np.arange(points)
    depth = np.full(points, depth_max)
    for power in range(1, depth_max + 1):
        depth = np.where(position % (2 ** power) == 0, depth_max - power, depth)
    return depth, depth_max


def advance(padded, diffuse, advect):
    centre = padded[1:-1]
    forward = padded[2:]
    backward = padded[:-2]
    result = centre + diffuse[0] * (forward - 2.0 * centre + backward) - advect[0] * (forward * forward - backward * backward) * 0.25
    for dimension in range(1, 6):
        forward = jnp.roll(centre, -1, dimension)
        backward = jnp.roll(centre, 1, dimension)
        result = result + diffuse[dimension] * (forward - 2.0 * centre + backward) - advect[dimension] * (forward * forward - backward * backward) * 0.25
    return result


def reference(state_field, levels, sign_bits):
    points = state_field.shape[1]
    depth_np, depth_max = level_depth(points)
    depth = jnp.asarray(depth_np, jnp.int32)

    def evolve_grid(item):
        values, level_row, sign_bit = item
        rates = jnp.exp2(level_row.astype(jnp.float32) - 4.0)
        diffuse = 0.08 * rates
        advect = 0.05 * rates
        for timestep in range(STEPS):
            padded = jnp.concatenate([values[-1:], values, values[:1]], 0)
            values = advance(padded, diffuse, advect)
        surplus = hierarchize(values.reshape(points, -1))
        sign_value = (2 * sign_bit - 1).astype(jnp.float32)
        return sign_value * surplus

    weighted = lax.map(evolve_grid, (state_field, levels, sign_bits))
    combined = jnp.sum(weighted, 0)

    def rebuild_grid(level_first):
        keep_mask = jnp.where(depth <= depth_max - 4 + level_first, 1.0, 0.0).astype(jnp.float32)
        rebuilt = dehierarchize(keep_mask[:, None] * combined)
        return rebuilt.reshape(state_field.shape[1:])

    return lax.map(rebuild_grid, levels[:, 0])
```

```python
import jax
import jax.numpy as jnp
from jax import lax
from jax.experimental import pallas as pl
from jax.experimental.pallas import tpu as pltpu
from jax.sharding import PartitionSpec as P

SCALE = 6.4
ROWS = 32
HALF = ROWS // 2


def devices_of(mesh):
    return mesh.shape["grid"], mesh.shape["tile"]


def layer_update(read_f, read_g, read_v, coef, masks, own, other, emit):
    low, first, last = masks
    centre, rate = coef
    for d2 in range(2):
        for d3 in range(4):
            rows = [own + d2 * 8 + d3 * 2 + a for a in range(2)]
            up2 = [(own + 8 if d2 == 0 else other) + d3 * 2 + a for a in range(2)]
            down2 = [(other + 8 if d2 == 0 else own) + d3 * 2 + a for a in range(2)]
            up3 = [own + d2 * 8 + (d3 + 1) % 4 * 2 + a for a in range(2)]
            down3 = [own + d2 * 8 + (d3 + 3) % 4 * 2 + a for a in range(2)]
            f = [read_f(0, row) for row in rows]
            g = [read_g(0, row) for row in rows]
            turned = [pltpu.roll(f[a] + g[1 - a], 4, 0) for a in range(2)]
            for a in range(2):
                total = centre * read_v(0, rows[a])
                total += rate[0] * (read_f(1, rows[a]) + read_g(-1, rows[a]))
                total += rate[1] * (read_f(0, up2[a]) + read_g(0, down2[a]))
                total += rate[2] * (read_f(0, up3[a]) + read_g(0, down3[a]))
                total += rate[3] * jnp.where(low, turned[a], turned[1 - a])
                ahead = jnp.where(last, pltpu.roll(f[a], 3, 0), pltpu.roll(f[a], 7, 0))
                behind = jnp.where(first, pltpu.roll(g[a], 5, 0), pltpu.roll(g[a], 1, 0))
                total += rate[4] * (ahead + behind)
                total += rate[5] * (pltpu.roll(f[a], 127, 1) + pltpu.roll(g[a], 1, 1))
                emit(d2 * 8 + d3 * 2 + a, rows[a], total)


def lane_masks():
    sub = lax.broadcasted_iota(jnp.int32, (8, 128), 0)
    return sub < 4, sub % 4 == 0, sub % 4 == 3


def coefficients(rates_ref):
    rate = [0.08 * rates_ref[d] for d in range(6)]
    total = rate[0] + rate[1] + rate[2] + rate[3] + rate[4] + rate[5]
    return 1.0 - 2.0 * total, rate


def put(vs, fs, gs, slot, layer, row, v):
    q = v * v
    vs[slot, layer, row] = v
    fs[slot, layer, row] = v - q
    gs[slot, layer, row] = v + q


def load_layer(vs, fs, gs, slot, layer, source, index, scale):
    for row in range(ROWS):
        v = source[index, row]
        put(vs, fs, gs, slot, layer, row, v * scale if scale is not None else v)


def step_layer(vs, fs, gs, slot, layer, coef, masks):
    for half in range(2):
        layer_update(
            lambda dx, row: fs[slot, layer + dx, row],
            lambda dx, row: gs[slot, layer + dx, row],
            lambda dx, row: vs[slot, layer + dx, row],
            coef, masks, half * HALF, (1 - half) * HALF,
            lambda at, row, v: put(vs, fs, gs, 1 - slot, layer, row, v),
        )


def last_layer(vs, fs, gs, slot, layer, coef, masks, core, sign, keep, send, out):
    for part, ref in ((0, keep), (1, send)):
        own = (core ^ part) * HALF

        def emit(at, row, v, ref=ref):
            ref[out, at] = v * sign

        layer_update(
            lambda dx, row: fs[slot, layer + dx, row],
            lambda dx, row: gs[slot, layer + dx, row],
            lambda dx, row: vs[slot, layer + dx, row],
            coef, masks, own, HALF - own, emit,
        )


def loop(low, high, body):
    lax.fori_loop(low, high, lambda i, carry: (body(i), carry)[1], 0)


def middle_kernel(rates, scalars, u, keep, send, edge_l, edge_r, vs, fs, gs):
    coef, masks = coefficients(rates), lane_masks()
    loop(0, 16, lambda i: load_layer(vs, fs, gs, 0, i, u, i, 1.0 / SCALE))
    for step in range(1, 4):
        slot = (step - 1) % 2
        loop(step, 16 - step, lambda i, s=slot: step_layer(vs, fs, gs, s, i, coef, masks))
        for k in range(2):
            edge_l[2 * (step - 1) + k] = vs[1 - slot, step + k]
            edge_r[2 * (step - 1) + k] = vs[1 - slot, 14 - step + k]
    core, sign = scalars[0], (scalars[1] * 2 - 1).astype(jnp.float32) * SCALE
    loop(0, 8, lambda i: last_layer(vs, fs, gs, 1, i + 4, coef, masks, core, sign, keep, send, i))


def outer_kernel(rates, scalars, u, halo_l, halo_r, edge_l, edge_r, keep, send, vs, fs, gs):
    coef, masks = coefficients(rates), lane_masks()
    inv = 1.0 / SCALE
    loop(0, 4, lambda i: load_layer(vs, fs, gs, 0, i, halo_l, i, inv))
    loop(0, 2, lambda i: load_layer(vs, fs, gs, 0, 4 + i, u, i, inv))
    loop(0, 2, lambda i: load_layer(vs, fs, gs, 0, 13 + i, u, 14 + i, inv))
    loop(0, 5, lambda i: load_layer(vs, fs, gs, 0, 15 + i, halo_r, i, inv))
    for step in range(1, 4):
        slot = (step - 1) % 2
        loop(step, step + 4, lambda i, s=slot: step_layer(vs, fs, gs, s, i, coef, masks))
        loop(15 - step, 20 - step, lambda i, s=slot: step_layer(vs, fs, gs, s, i, coef, masks))
        for k in range(2):
            load_layer(vs, fs, gs, 1 - slot, 4 + step + k, edge_l, 2 * (step - 1) + k, None)
            load_layer(vs, fs, gs, 1 - slot, 13 - step + k, edge_r, 2 * (step - 1) + k, None)
    core, sign = scalars[0], (scalars[1] * 2 - 1).astype(jnp.float32) * SCALE
    loop(0, 4, lambda i: last_layer(vs, fs, gs, 1, i + 4, coef, masks, core, sign, keep, send, i))
    loop(0, 5, lambda i: last_layer(vs, fs, gs, 1, i + 11, coef, masks, core, sign, keep, send, i + 4))


def rebuild_kernel(scalars, mid_own, mid_other, out_own, out_other, result, full):
    core, shift = scalars[0], scalars[2]
    spacing = jnp.left_shift(jnp.int32(1), shift)
    for half, mid, outer in ((core, mid_own, out_own), (1 - core, mid_other, out_other)):
        rows = pl.ds(half * HALF, HALF)

        def place(i, half=half, mid=mid, outer=outer, rows=rows):
            full[4 + i, rows] = mid[i]

        loop(0, 8, place)
        for i in range(4):
            full[i, rows] = outer[i]
        for i in range(5):
            full[12 + i, rows] = outer[4 + i]

    def one(i):
        anchor = jnp.left_shift(jnp.right_shift(i, shift), shift)
        right = (i - anchor).astype(jnp.float32) / spacing.astype(jnp.float32)
        result[i] = full[anchor] * (1.0 - right) + full[anchor + spacing] * right

    loop(0, 16, one)


VMEM = pl.BlockSpec(memory_space=pltpu.VMEM)
SMEM = pl.BlockSpec(memory_space=pltpu.SMEM)
F32 = jnp.float32


def shape(*dims):
    return jax.ShapeDtypeStruct(dims, F32)


def call(kernel, name, n_smem, n_in, outs, scratch, layers):
    work = layers * ROWS * 8 * 128
    return pl.pallas_call(
        kernel,
        name=name,
        out_shape=outs,
        in_specs=[SMEM] * n_smem + [VMEM] * n_in,
        out_specs=jax.tree.map(lambda _: VMEM, outs),
        scratch_shapes=scratch,
        cost_estimate=pl.CostEstimate(flops=work * 40, bytes_accessed=work * 8, transcendentals=0),
        compiler_params=pltpu.CompilerParams(vmem_limit_bytes=48 << 20),
    )


def on_device(grids, tiles, state_field, levels, sign_bits):
    u = state_field.reshape(16, ROWS, 8, 128)

    def flat(y, core, rest):
        return ((y // 2) * 2 + core) * tiles + (y % 2) * (tiles // 2) + rest

    every = [(y, c, r) for y in range(grids) for c in range(2) for r in range(tiles // 2)]
    to_core = [(flat(y, c, r), flat(y, 1 - c, r)) for y, c, r in every]
    to_far = [(flat(y, c, r), flat((y + 2) % 4, c, r)) for y, c, r in every]

    def send(x, pairs):
        return lax.ppermute(x, ("grid", "tile"), pairs)

    halo_l = lax.ppermute(u[12:], "tile", [(i, (i + 1) % tiles) for i in range(tiles)])
    halo_r = lax.ppermute(u[:5], "tile", [((i + 1) % tiles, i) for i in range(tiles)])

    rates = jnp.exp2(levels[0].astype(F32) - 4.0)
    core = lax.axis_index("grid") % 2
    scalars = jnp.stack([core.astype(jnp.int32), sign_bits[0], 4 - levels[0, 0]])

    def buffers(n):
        return [pltpu.VMEM((2, n, ROWS, 8, 128), F32)] * 3

    keep_m, send_m, edge_l, edge_r = call(
        middle_kernel, "middle", 2, 1,
        (shape(8, HALF, 8, 128), shape(8, HALF, 8, 128), shape(6, ROWS, 8, 128), shape(6, ROWS, 8, 128)),
        buffers(16), 44,
    )(rates, scalars, u)
    part_m = keep_m + send(send_m, to_core)
    far_m = send(part_m, to_far)
    keep_o, send_o = call(
        outer_kernel, "outer", 2, 5, (shape(9, HALF, 8, 128), shape(9, HALF, 8, 128)), buffers(20), 36,
    )(rates, scalars, u, halo_l, halo_r, edge_l, edge_r)
    part_o = keep_o + send(send_o, to_core)
    far_o = send(part_o, to_far)
    own_m = part_m + far_m
    other_m = send(own_m, to_core)
    own_o = part_o + far_o
    other_o = send(own_o, to_core)
    result = call(
        rebuild_kernel, "rebuild", 1, 4, shape(16, ROWS, 8, 128), [pltpu.VMEM((17, ROWS, 8, 128), F32)], 2,
    )(scalars, own_m, other_m, own_o, other_o)
    return result.reshape(state_field.shape)


def solution(mesh):
    grids, tiles = devices_of(mesh)
    placed = (P("grid", "tile", None, None, None, None, None), P("grid", None), P("grid"))
    return jax.shard_map(
        lambda *args: on_device(grids, tiles, *args),
        mesh=mesh,
        in_specs=placed,
        out_specs=P("grid", "tile", None, None, None, None, None),
        check_vma=False,
    )
```

```python
import functools

import jax
import jax.numpy as jnp
from jax import lax
from jax.experimental import pallas as pl
from jax.experimental.pallas import tpu as pltpu
from jax.sharding import PartitionSpec as P

SCALE = 6.4
ROWS = 32
HALF = ROWS // 2


def devices_of(mesh):
    return mesh.shape["grid"], mesh.shape["tile"]


def layer_update(src, layer, coef, masks, own, other, emit):
    vs, fs, gs = src
    low, ahead, behind = masks
    centre, rate = coef
    for d2 in range(2):
        base = own + d2 * 8
        above = own + 8 if d2 == 0 else other
        below = other + 8 if d2 == 0 else own
        f = [fs[layer, base + k] for k in range(8)]
        g = [gs[layer, base + k] for k in range(8)]
        for k in range(8):
            total = centre * vs[layer, base + k]
            total += rate[0] * (fs[layer + 1, base + k] + gs[layer - 1, base + k])
            total += rate[1] * (fs[layer, above + k] + gs[layer, below + k])
            total += rate[2] * (f[(k + 2) % 8] + g[(k + 6) % 8])
            pair = k ^ 1
            total += rate[3] * jnp.where(
                low, pltpu.roll(f[k] + g[pair], 4, 0), pltpu.roll(f[pair] + g[k], 4, 0)
            )
            total += rate[4] * (
                jnp.take_along_axis(f[k], ahead, axis=0, mode="promise_in_bounds")
                + jnp.take_along_axis(g[k], behind, axis=0, mode="promise_in_bounds")
            )
            total += rate[5] * (pltpu.roll(f[k], 127, 1) + pltpu.roll(g[k], 1, 1))
            emit(d2 * 8 + k, base + k, total)


def lane_masks():
    sub = lax.broadcasted_iota(jnp.int32, (8, 128), 0)
    group = sub - sub % 4
    return sub < 4, group + (sub + 1) % 4, group + (sub + 3) % 4


def coefficients(levels):
    rate = [0.08 / 16.0 * jnp.left_shift(jnp.int32(1), levels[0, d]).astype(jnp.float32) for d in range(6)]
    total = rate[0] + rate[1] + rate[2] + rate[3] + rate[4] + rate[5]
    return 1.0 - 2.0 * total, rate


def put(dst, layer, row, v):
    vs, fs, gs = dst
    q = v * v
    vs[layer, row] = v
    fs[layer, row] = v - q
    gs[layer, row] = v + q


def load_layer(dst, layer, source, index, scale):
    for row in range(ROWS):
        v = source[index, row]
        put(dst, layer, row, v * scale if scale is not None else v)


def step_layer(src, dst, layer, coef, masks):
    for half in range(2):
        layer_update(
            src, layer, coef, masks, half * HALF, (1 - half) * HALF,
            lambda at, row, v: put(dst, layer, row, v),
        )


def last_layer(src, layer, coef, masks, core, sign, keep, send, out):
    for part, ref in ((0, keep), (1, send)):
        own = (core ^ part) * HALF

        def emit(at, row, v, ref=ref):
            ref[out, at] = v * sign

        layer_update(src, layer, coef, masks, own, HALF - own, emit)


def loop(low, high, body):
    def two(i, carry):
        body(low + 2 * i)
        body(low + 2 * i + 1)
        return carry

    lax.fori_loop(0, (high - low) // 2, two, 0)
    if (high - low) % 2:
        body(high - 1)


def middle_kernel(levels, signs, core_ref, u, keep_a, send_a, keep_b, send_b, edge_l, edge_r, *scratch):
    bufs = scratch[:3], scratch[3:]
    coef, masks = coefficients(levels), lane_masks()
    loop(0, 16, lambda i: load_layer(bufs[0], i, u, i, 1.0 / SCALE))
    for step in range(1, 4):
        src, dst = bufs[(step - 1) % 2], bufs[step % 2]
        loop(step, 16 - step, lambda i, s=src, d=dst: step_layer(s, d, i, coef, masks))
        for k in range(2):
            edge_l[2 * (step - 1) + k] = dst[0][step + k]
            edge_r[2 * (step - 1) + k] = dst[0][14 - step + k]
    core, sign = core_ref[0], (signs[0] * 2 - 1).astype(jnp.float32) * SCALE
    loop(0, 4, lambda i: last_layer(bufs[1], i + 4, coef, masks, core, sign, keep_a, send_a, i))
    loop(0, 4, lambda i: last_layer(bufs[1], i + 8, coef, masks, core, sign, keep_b, send_b, i))


def outer_kernel(levels, signs, core_ref, u, left, right, edge_l, edge_r, keep_l, send_l, keep_r, send_r, *scratch):
    bufs = scratch[:3], scratch[3:]
    coef, masks = coefficients(levels), lane_masks()
    for at, source, first, count, scale in (
        (0, left, 0, 4, None), (4, u, 0, 2, 1.0 / SCALE), (13, u, 14, 2, 1.0 / SCALE), (15, right, 0, 4, None)
    ):
        loop(
            0, count,
            lambda i, at=at, source=source, first=first, scale=scale: load_layer(bufs[0], at + i, source, first + i, scale),
        )
    for step in range(1, 4):
        src, dst = bufs[(step - 1) % 2], bufs[step % 2]
        loop(step, step + 4, lambda i, s=src, d=dst: step_layer(s, d, i, coef, masks))
        loop(15 - step, 19 - step, lambda i, s=src, d=dst: step_layer(s, d, i, coef, masks))
        for k in range(2):
            load_layer(dst, 4 + step + k, edge_l, 2 * (step - 1) + k, None)
            load_layer(dst, 13 - step + k, edge_r, 2 * (step - 1) + k, None)
    core, sign = core_ref[0], (signs[0] * 2 - 1).astype(jnp.float32) * SCALE
    loop(0, 4, lambda i: last_layer(bufs[1], i + 4, coef, masks, core, sign, keep_l, send_l, i))
    loop(0, 4, lambda i: last_layer(bufs[1], i + 11, coef, masks, core, sign, keep_r, send_r, i))


def interpolate(levels, points, first, read, write):
    for level in range(1, 5):

        @pl.when(levels[0, 0] == level)
        def _(space=1 << (4 - level)):
            for row in range(first, first + GROUP):
                kept = {}

                def keep(p, row=row, kept=kept):
                    if p not in kept:
                        kept[p] = read(p, row)
                    return kept[p]

                for p in points:
                    anchor, share = p // space * space, p % space / space
                    v = keep(anchor)
                    if share:
                        v = v * (1.0 - share) + keep(anchor + space) * share
                    write(p, row, v)


GROUP = 4


def early_kernel(levels, core_ref, own_l, own_m, other_l, other_m, result, rows, sems):
    copies = []
    for part, (l, m) in enumerate(((own_l, own_m), (other_l, other_m))):
        for first in range(0, HALF, GROUP):

            def write(p, row, v, part=part):
                rows[part, p, row] = v

            interpolate(levels, range(8), first, lambda p, row, l=l, m=m: l[p, row] if p < 4 else m[p - 4, row], write)
            copies.append(pltpu.make_async_copy(
                rows.at[part, :, pl.ds(first, GROUP)],
                result.at[pl.ds(0, 8), pl.ds((core_ref[0] ^ part) * HALF + first, GROUP)],
                sems.at[len(copies)],
            ))
            copies[-1].start()
    for copy in copies:
        copy.wait()


def late_kernel(which, levels, core_ref, m, r, _, result, rows, sems):
    copies = []

    def write(p, row, v):
        rows[p - 8, row] = v

    for first in range(0, HALF, GROUP):
        interpolate(levels, range(8, 16), first, lambda p, row: m[p - 4, row] if p < 12 else r[p - 12, row], write)
        copies.append(pltpu.make_async_copy(
            rows.at[:, pl.ds(first, GROUP)],
            result.at[pl.ds(8, 8), pl.ds((core_ref[0] ^ which) * HALF + first, GROUP)],
            sems.at[len(copies)],
        ))
        copies[-1].start()
    for copy in copies:
        copy.wait()


VMEM = pl.BlockSpec(memory_space=pltpu.VMEM)
ANY = pl.BlockSpec(memory_space=pl.ANY)
SMEM = pl.BlockSpec(memory_space=pltpu.SMEM)
F32 = jnp.float32


def shape(*dims):
    return jax.ShapeDtypeStruct(dims, F32)


def call(kernel, name, specs, out_specs, outs, scratch, cost_us, aliases={}, vmem=24):
    return pl.pallas_call(
        kernel,
        name=name,
        out_shape=outs,
        in_specs=specs,
        out_specs=out_specs,
        scratch_shapes=scratch,
        input_output_aliases=aliases,
        cost_estimate=pl.CostEstimate(flops=0, bytes_accessed=int(cost_us * 3.69e6), transcendentals=0),
        compiler_params=pltpu.CompilerParams(vmem_limit_bytes=vmem << 20),
    )


def on_device(grids, tiles, state_field, levels, sign_bits):
    u = state_field.reshape(16, ROWS, 8, 128)

    def flat(y, core, rest):
        return ((y // 2) * 2 + core) * tiles + (y % 2) * (tiles // 2) + rest

    every = [(y, c, r) for y in range(grids) for c in range(2) for r in range(tiles // 2)]
    to_core = [(flat(y, c, r), flat(y, 1 - c, r)) for y, c, r in every]
    to_far = [(flat(y, c, r), flat((y + 2) % 4, c, r)) for y, c, r in every]

    def send(x, pairs):
        return lax.ppermute(x, ("grid", "tile"), pairs)

    tail, head = u[12:] * (1.0 / SCALE), u[:4] * (1.0 / SCALE)
    up = [(i, (i + 1) % tiles) for i in range(tiles)]
    down = [((i + 1) % tiles, i) for i in range(tiles)]
    left, right = lax.ppermute(tail, "tile", up), lax.ppermute(head, "tile", down)

    core = (lax.axis_index("grid") & 1).astype(jnp.int32).reshape(1)

    def buffers(n):
        return [pltpu.VMEM((n, ROWS, 8, 128), F32)] * 6

    half, edge = shape(4, HALF, 8, 128), shape(6, ROWS, 8, 128)
    keep_a, send_a, keep_b, send_b, edge_l, edge_r = call(
        middle_kernel, "middle", [SMEM] * 3 + [VMEM], (VMEM,) * 6, (half,) * 4 + (edge,) * 2, buffers(16), 6, vmem=16,
    )(levels, sign_bits, core, u)
    got_a, got_b = send(send_a, to_core), send(send_b, to_core)
    got_a, got_b, left, right = lax.optimization_barrier((got_a, got_b, left, right))
    part_m = jnp.concatenate([keep_a + got_a, keep_b + got_b])
    part_m, left, right = lax.optimization_barrier((part_m, left, right))
    far_m = send(part_m, to_far)
    keep_l, send_l, keep_r, send_r = call(
        outer_kernel, "outer", [SMEM] * 3 + [VMEM] * 5, (VMEM,) * 4, (half,) * 4, buffers(19), 6, vmem=20,
    )(levels, sign_bits, core, u, left, right, edge_l, edge_r)
    part_l, part_r = keep_l + send(send_l, to_core), keep_r + send(send_r, to_core)
    far_l = send(part_l, to_far)
    part_r, far_m = lax.optimization_barrier((part_r, far_m))
    far_r = send(part_r, to_far)
    own_l = part_l + far_l
    following = lax.ppermute(own_l[:1], "tile", down)
    other_l = send(own_l, to_core)
    own_m = part_m + far_m
    other_m = send(own_m, to_core)
    whole = shape(16, ROWS, 8, 128)
    result = call(
        early_kernel, "early", [SMEM] * 2 + [VMEM] * 4, ANY, whole,
        [pltpu.VMEM((2, 8, HALF, 8, 128), F32), pltpu.SemaphoreType.DMA((2 * HALF // GROUP,))], 1.5, vmem=8,
    )(levels, core, own_l, own_m, other_l, other_m)
    own_r = jnp.concatenate([part_r + far_r, following])
    own_r, result = lax.optimization_barrier((own_r, result))
    other_r = send(own_r, to_core)
    for which, m, r in ((0, own_m, own_r), (1, other_m, other_r)):
        result = call(
            functools.partial(late_kernel, which), ("late_own", "late_other")[which], [SMEM] * 2 + [VMEM] * 2 + [ANY],
            ANY, whole, [pltpu.VMEM((8, HALF, 8, 128), F32), pltpu.SemaphoreType.DMA((HALF // GROUP,))], 1, {4: 0}, vmem=8,
        )(levels, core, m, r, result)
    return result.reshape(state_field.shape)


def solution(mesh):
    grids, tiles = devices_of(mesh)
    placed = (P("grid", "tile", None, None, None, None, None), P("grid", None), P("grid"))
    return jax.shard_map(
        lambda *args: on_device(grids, tiles, *args),
        mesh=mesh,
        in_specs=placed,
        out_specs=P("grid", "tile", None, None, None, None, None),
        check_vma=False,
    )
```

```python
import functools

import jax
import jax.numpy as jnp
from jax import lax
from jax.experimental import pallas as pl
from jax.experimental.pallas import tpu as pltpu
from jax.sharding import PartitionSpec as P

SCALE = 6.4
ROWS = 32
HALF = ROWS // 2


def devices_of(mesh):
    return mesh.shape["grid"], mesh.shape["tile"]


def layer_update(src, layer, coef, masks, own, other, emit):
    vs, fs, gs = src
    low, ahead, behind = masks
    centre, rate = coef
    for d2 in range(2):
        base = own + d2 * 8
        above = own + 8 if d2 == 0 else other
        below = other + 8 if d2 == 0 else own
        f = [fs[layer, base + k] for k in range(8)]
        g = [gs[layer, base + k] for k in range(8)]
        for k in range(8):
            total = centre * vs[layer, base + k]
            total += rate[0] * (fs[layer + 1, base + k] + gs[layer - 1, base + k])
            total += rate[1] * (fs[layer, above + k] + gs[layer, below + k])
            total += rate[2] * (f[(k + 2) % 8] + g[(k + 6) % 8])
            pair = k ^ 1
            total += rate[3] * jnp.where(
                low, pltpu.roll(f[k] + g[pair], 4, 0), pltpu.roll(f[pair] + g[k], 4, 0)
            )
            total += rate[4] * (
                jnp.take_along_axis(f[k], ahead, axis=0, mode="promise_in_bounds")
                + jnp.take_along_axis(g[k], behind, axis=0, mode="promise_in_bounds")
            )
            total += rate[5] * (pltpu.roll(f[k], 127, 1) + pltpu.roll(g[k], 1, 1))
            emit(d2 * 8 + k, base + k, total)


def lane_masks():
    sub = lax.broadcasted_iota(jnp.int32, (8, 128), 0)
    group = sub - sub % 4
    return sub < 4, group + (sub + 1) % 4, group + (sub + 3) % 4


def coefficients(levels):
    rate = [0.08 / 16.0 * jnp.left_shift(jnp.int32(1), levels[0, d]).astype(jnp.float32) for d in range(6)]
    total = rate[0] + rate[1] + rate[2] + rate[3] + rate[4] + rate[5]
    return 1.0 - 2.0 * total, rate


def put(dst, layer, row, v):
    vs, fs, gs = dst
    q = v * v
    vs[layer, row] = v
    fs[layer, row] = v - q
    gs[layer, row] = v + q


def load_layer(dst, layer, source, index, scale):
    for row in range(ROWS):
        v = source[index, row]
        put(dst, layer, row, v * scale if scale is not None else v)


def step_layer(src, dst, layer, coef, masks):
    for half in range(2):
        layer_update(
            src, layer, coef, masks, half * HALF, (1 - half) * HALF,
            lambda at, row, v: put(dst, layer, row, v),
        )


def last_layer(src, layer, coef, masks, core, sign, keep, send, out):
    for part, ref in ((0, keep), (1, send)):
        own = (core ^ part) * HALF

        def emit(at, row, v, ref=ref):
            ref[out, at] = v * sign

        layer_update(src, layer, coef, masks, own, HALF - own, emit)


def loop(low, high, body):
    def two(i, carry):
        body(low + 2 * i)
        body(low + 2 * i + 1)
        return carry

    lax.fori_loop(0, (high - low) // 2, two, 0)
    if (high - low) % 2:
        body(high - 1)


def middle_kernel(levels, signs, core_ref, u, keep_a, send_a, keep_b, send_b, edge_l, edge_r, *scratch):
    bufs = scratch[:3], scratch[3:]
    coef, masks = coefficients(levels), lane_masks()
    loop(0, 16, lambda i: load_layer(bufs[0], i, u, i, 1.0 / SCALE))
    for step in range(1, 4):
        src, dst = bufs[(step - 1) % 2], bufs[step % 2]
        loop(step, 16 - step, lambda i, s=src, d=dst: step_layer(s, d, i, coef, masks))
        for k in range(2):
            edge_l[2 * (step - 1) + k] = dst[0][step + k]
            edge_r[2 * (step - 1) + k] = dst[0][14 - step + k]
    core, sign = core_ref[0], (signs[0] * 2 - 1).astype(jnp.float32) * SCALE
    loop(0, 6, lambda i: last_layer(bufs[1], i + 4, coef, masks, core, sign, keep_a, send_a, i))
    loop(0, 2, lambda i: last_layer(bufs[1], i + 10, coef, masks, core, sign, keep_b, send_b, i))


def outer_kernel(levels, signs, core_ref, u, left, right, edge_l, edge_r, keep_l, send_l, keep_r, send_r, *scratch):
    bufs = scratch[:3], scratch[3:]
    coef, masks = coefficients(levels), lane_masks()
    for at, source, first, count, scale in (
        (0, left, 0, 4, None), (4, u, 0, 2, 1.0 / SCALE), (13, u, 14, 2, 1.0 / SCALE), (15, right, 0, 4, None)
    ):
        loop(
            0, count,
            lambda i, at=at, source=source, first=first, scale=scale: load_layer(bufs[0], at + i, source, first + i, scale),
        )
    for step in range(1, 4):
        src, dst = bufs[(step - 1) % 2], bufs[step % 2]
        loop(step, step + 4, lambda i, s=src, d=dst: step_layer(s, d, i, coef, masks))
        loop(15 - step, 19 - step, lambda i, s=src, d=dst: step_layer(s, d, i, coef, masks))
        for k in range(2):
            load_layer(dst, 4 + step + k, edge_l, 2 * (step - 1) + k, None)
            load_layer(dst, 13 - step + k, edge_r, 2 * (step - 1) + k, None)
    core, sign = core_ref[0], (signs[0] * 2 - 1).astype(jnp.float32) * SCALE
    loop(0, 4, lambda i: last_layer(bufs[1], i + 4, coef, masks, core, sign, keep_l, send_l, i))
    loop(0, 4, lambda i: last_layer(bufs[1], i + 11, coef, masks, core, sign, keep_r, send_r, i))


def interpolate(levels, points, first, read, write):
    for level in range(1, 5):

        @pl.when(levels[0, 0] == level)
        def _(space=1 << (4 - level)):
            for row in range(first, first + GROUP):
                kept = {}

                def keep(p, row=row, kept=kept):
                    if p not in kept:
                        kept[p] = read(p, row)
                    return kept[p]

                for p in points:
                    anchor, share = p // space * space, p % space / space
                    v = keep(anchor)
                    if share:
                        v = v * (1.0 - share) + keep(anchor + space) * share
                    write(p, row, v)


GROUP = 4


def early_kernel(levels, core_ref, own_l, own_m, other_l, other_m, result, rows, sems):
    copies = []
    for part, (l, m) in enumerate(((own_l, own_m), (other_l, other_m))):
        for first in range(0, HALF, GROUP):

            def write(p, row, v, part=part):
                rows[part, p, row] = v

            interpolate(levels, range(8), first, lambda p, row, l=l, m=m: l[p, row] if p < 4 else m[p - 4, row], write)
            copies.append(pltpu.make_async_copy(
                rows.at[part, :, pl.ds(first, GROUP)],
                result.at[pl.ds(0, 8), pl.ds((core_ref[0] ^ part) * HALF + first, GROUP)],
                sems.at[len(copies)],
            ))
            copies[-1].start()
    for copy in copies:
        copy.wait()


def late_kernel(which, levels, core_ref, m, r, _, result, rows, sems):
    copies = []

    def write(p, row, v):
        rows[p - 8, row] = v

    for first in range(0, HALF, GROUP):
        interpolate(levels, range(8, 16), first, lambda p, row: m[p - 4, row] if p < 10 else r[p - 10, row], write)
        copies.append(pltpu.make_async_copy(
            rows.at[:, pl.ds(first, GROUP)],
            result.at[pl.ds(8, 8), pl.ds((core_ref[0] ^ which) * HALF + first, GROUP)],
            sems.at[len(copies)],
        ))
        copies[-1].start()
    for copy in copies:
        copy.wait()


VMEM = pl.BlockSpec(memory_space=pltpu.VMEM)
ANY = pl.BlockSpec(memory_space=pl.ANY)
SMEM = pl.BlockSpec(memory_space=pltpu.SMEM)
F32 = jnp.float32


def shape(*dims):
    return jax.ShapeDtypeStruct(dims, F32)


def call(kernel, name, specs, out_specs, outs, scratch, cost_us, aliases={}, vmem=24):
    return pl.pallas_call(
        kernel,
        name=name,
        out_shape=outs,
        in_specs=specs,
        out_specs=out_specs,
        scratch_shapes=scratch,
        input_output_aliases=aliases,
        cost_estimate=pl.CostEstimate(flops=0, bytes_accessed=int(cost_us * 3.69e6), transcendentals=0),
        compiler_params=pltpu.CompilerParams(vmem_limit_bytes=vmem << 20),
    )


def on_device(grids, tiles, state_field, levels, sign_bits):
    u = state_field.reshape(16, ROWS, 8, 128)

    def flat(y, core, rest):
        return ((y // 2) * 2 + core) * tiles + (y % 2) * (tiles // 2) + rest

    every = [(y, c, r) for y in range(grids) for c in range(2) for r in range(tiles // 2)]
    to_core = [(flat(y, c, r), flat(y, 1 - c, r)) for y, c, r in every]
    to_far = [(flat(y, c, r), flat((y + 2) % 4, c, r)) for y, c, r in every]

    def send(x, pairs):
        return lax.ppermute(x, ("grid", "tile"), pairs)

    tail, head = u[12:] * (1.0 / SCALE), u[:4] * (1.0 / SCALE)
    up = [(i, (i + 1) % tiles) for i in range(tiles)]
    down = [((i + 1) % tiles, i) for i in range(tiles)]
    left, right = lax.ppermute(tail, "tile", up), lax.ppermute(head, "tile", down)

    core = (lax.axis_index("grid") & 1).astype(jnp.int32).reshape(1)

    def buffers(n):
        return [pltpu.VMEM((n, ROWS, 8, 128), F32)] * 6

    half, edge = shape(4, HALF, 8, 128), shape(6, ROWS, 8, 128)
    keep_a, send_a, keep_b, send_b, edge_l, edge_r = call(
        middle_kernel, "middle", [SMEM] * 3 + [VMEM], (VMEM,) * 6, (shape(6, HALF, 8, 128),) * 2 + (shape(2, HALF, 8, 128),) * 2 + (edge,) * 2, buffers(16), 6, vmem=16,
    )(levels, sign_bits, core, u)
    got_a, got_b = send(send_a, to_core), send(send_b, to_core)
    part_m, part_b = keep_a + got_a, keep_b + got_b
    part_m, edge_l, edge_r = lax.optimization_barrier((part_m, edge_l, edge_r))
    far_m = send(part_m, to_far)
    keep_l, send_l, keep_r, send_r = call(
        outer_kernel, "outer", [SMEM] * 3 + [VMEM] * 5, (VMEM,) * 4, (half,) * 4, buffers(19), 6, vmem=20,
    )(levels, sign_bits, core, u, left, right, edge_l, edge_r)
    part_l = keep_l + send(send_l, to_core)
    part_r = jnp.concatenate([part_b, keep_r + send(send_r, to_core)])
    far_l = send(part_l, to_far)
    part_r, far_m = lax.optimization_barrier((part_r, far_m))
    far_r = send(part_r, to_far)
    own_l = part_l + far_l
    following = lax.ppermute(own_l[:1], "tile", down)
    other_l = send(own_l, to_core)
    own_m = part_m + far_m
    other_m = send(own_m, to_core)
    whole = shape(16, ROWS, 8, 128)
    result = call(
        early_kernel, "early", [SMEM] * 2 + [VMEM] * 4, ANY, whole,
        [pltpu.VMEM((2, 8, HALF, 8, 128), F32), pltpu.SemaphoreType.DMA((2 * HALF // GROUP,))], 1.5, vmem=8,
    )(levels, core, own_l, own_m, other_l, other_m)
    far_r, following, result = lax.optimization_barrier((far_r, following, result))
    own_r = jnp.concatenate([part_r + far_r, following])
    other_r = send(own_r, to_core)
    for which, m, r in ((0, own_m, own_r), (1, other_m, other_r)):
        result = call(
            functools.partial(late_kernel, which), ("late_own", "late_other")[which], [SMEM] * 2 + [VMEM] * 2 + [ANY],
            ANY, whole, [pltpu.VMEM((8, HALF, 8, 128), F32), pltpu.SemaphoreType.DMA((HALF // GROUP,))], 1, {4: 0}, vmem=8,
        )(levels, core, m, r, result)
    return result.reshape(state_field.shape)


def solution(mesh):
    grids, tiles = devices_of(mesh)
    placed = (P("grid", "tile", None, None, None, None, None), P("grid", None), P("grid"))
    return jax.shard_map(
        lambda *args: on_device(grids, tiles, *args),
        mesh=mesh,
        in_specs=placed,
        out_specs=P("grid", "tile", None, None, None, None, None),
        check_vma=False,
    )
```

```python
import functools

import jax
import jax.numpy as jnp
from jax import lax
from jax.experimental import pallas as pl
from jax.experimental.pallas import tpu as pltpu
from jax.sharding import PartitionSpec as P

SCALE = 6.4
ROWS = 32
HALF = ROWS // 2


def devices_of(mesh):
    return mesh.shape["grid"], mesh.shape["tile"]


def layer_update(src, layer, coef, masks, own, other, emit):
    vs, fs, gs = src
    low, ahead, behind = masks
    centre, rate = coef
    for d2 in range(2):
        base = own + d2 * 8
        above = own + 8 if d2 == 0 else other
        below = other + 8 if d2 == 0 else own
        f = [fs[layer, base + k] for k in range(8)]
        g = [gs[layer, base + k] for k in range(8)]
        for k in range(8):
            total = centre * vs[layer, base + k]
            total += rate[0] * (fs[layer + 1, base + k] + gs[layer - 1, base + k])
            total += rate[1] * (fs[layer, above + k] + gs[layer, below + k])
            total += rate[2] * (f[(k + 2) % 8] + g[(k + 6) % 8])
            pair = k ^ 1
            total += rate[3] * jnp.where(
                low, pltpu.roll(f[k] + g[pair], 4, 0), pltpu.roll(f[pair] + g[k], 4, 0)
            )
            total += rate[4] * (
                jnp.take_along_axis(f[k], ahead, axis=0, mode="promise_in_bounds")
                + jnp.take_along_axis(g[k], behind, axis=0, mode="promise_in_bounds")
            )
            total += rate[5] * (pltpu.roll(f[k], 127, 1) + pltpu.roll(g[k], 1, 1))
            emit(d2 * 8 + k, base + k, total)


def lane_masks():
    sub = lax.broadcasted_iota(jnp.int32, (8, 128), 0)
    group = sub - sub % 4
    return sub < 4, group + (sub + 1) % 4, group + (sub + 3) % 4


def coefficients(levels):
    rate = [0.08 / 16.0 * jnp.left_shift(jnp.int32(1), levels[0, d]).astype(jnp.float32) for d in range(6)]
    total = rate[0] + rate[1] + rate[2] + rate[3] + rate[4] + rate[5]
    return 1.0 - 2.0 * total, rate


def put(dst, layer, row, v):
    vs, fs, gs = dst
    q = v * v
    vs[layer, row] = v
    fs[layer, row] = v - q
    gs[layer, row] = v + q


def load_layer(dst, layer, source, index, scale):
    for row in range(ROWS):
        v = source[index, row]
        put(dst, layer, row, v * scale if scale is not None else v)


def step_layer(src, dst, layer, coef, masks):
    for half in range(2):
        layer_update(
            src, layer, coef, masks, half * HALF, (1 - half) * HALF,
            lambda at, row, v: put(dst, layer, row, v),
        )


def last_layer(src, layer, coef, masks, core, sign, keep, send, out):
    for part, ref in ((0, keep), (1, send)):
        own = (core ^ part) * HALF

        def emit(at, row, v, ref=ref):
            ref[out, at] = v * sign

        layer_update(src, layer, coef, masks, own, HALF - own, emit)


def loop(low, high, body, width=4):
    def several(i, carry):
        for j in range(width):
            body(low + width * i + j)
        return carry

    lax.fori_loop(0, (high - low) // width, several, 0)
    for i in range(high - (high - low) % width, high):
        body(i)


def middle_kernel(levels, signs, core_ref, u, keep_a, send_a, keep_b, send_b, edge_l, edge_r, *scratch):
    bufs = scratch[:3], scratch[3:]
    coef, masks = coefficients(levels), lane_masks()
    loop(0, 16, lambda i: load_layer(bufs[0], i, u, i, 1.0 / SCALE))
    for step in range(1, 4):
        src, dst = bufs[(step - 1) % 2], bufs[step % 2]
        loop(step, 16 - step, lambda i, s=src, d=dst: step_layer(s, d, i, coef, masks))
        for k in range(2):
            edge_l[2 * (step - 1) + k] = dst[0][step + k]
            edge_r[2 * (step - 1) + k] = dst[0][14 - step + k]
    core, sign = core_ref[0], (signs[0] * 2 - 1).astype(jnp.float32) * SCALE
    loop(0, 6, lambda i: last_layer(bufs[1], i + 4, coef, masks, core, sign, keep_a, send_a, i))
    loop(0, 2, lambda i: last_layer(bufs[1], i + 10, coef, masks, core, sign, keep_b, send_b, i))


def outer_kernel(levels, signs, core_ref, u, left, right, edge_l, edge_r, keep_l, send_l, keep_r, send_r, *scratch):
    bufs = scratch[:3], scratch[3:]
    coef, masks = coefficients(levels), lane_masks()
    for at, source, first, count, scale in (
        (0, left, 0, 4, None), (4, u, 0, 2, 1.0 / SCALE), (13, u, 14, 2, 1.0 / SCALE), (15, right, 0, 4, None)
    ):
        loop(
            0, count,
            lambda i, at=at, source=source, first=first, scale=scale: load_layer(bufs[0], at + i, source, first + i, scale),
        )
    for step in range(1, 4):
        src, dst = bufs[(step - 1) % 2], bufs[step % 2]
        for i in range(4):
            step_layer(src, dst, step + i, coef, masks)
            step_layer(src, dst, 15 - step + i, coef, masks)
        for k in range(2):
            load_layer(dst, 4 + step + k, edge_l, 2 * (step - 1) + k, None)
            load_layer(dst, 13 - step + k, edge_r, 2 * (step - 1) + k, None)
    core, sign = core_ref[0], (signs[0] * 2 - 1).astype(jnp.float32) * SCALE
    for i in range(4):
        last_layer(bufs[1], i + 4, coef, masks, core, sign, keep_l, send_l, i)
        last_layer(bufs[1], i + 11, coef, masks, core, sign, keep_r, send_r, i)


def interpolate(levels, points, first, read, write):
    for level in range(1, 5):

        @pl.when(levels[0, 0] == level)
        def _(space=1 << (4 - level)):
            for row in range(first, first + GROUP):
                kept = {}

                def keep(p, row=row, kept=kept):
                    if p not in kept:
                        kept[p] = read(p, row)
                    return kept[p]

                for p in points:
                    anchor, share = p // space * space, p % space / space
                    v = keep(anchor)
                    if share:
                        v = v * (1.0 - share) + keep(anchor + space) * share
                    write(p, row, v)


GROUP = 4


def early_kernel(levels, core_ref, own_l, own_m, other_l, other_m, result, rows, sems):
    copies = []
    for part, (l, m) in enumerate(((own_l, own_m), (other_l, other_m))):
        for first in range(0, HALF, GROUP):

            def write(p, row, v, part=part):
                rows[part, p, row] = v

            interpolate(levels, range(8), first, lambda p, row, l=l, m=m: l[p, row] if p < 4 else m[p - 4, row], write)
            copies.append(pltpu.make_async_copy(
                rows.at[part, :, pl.ds(first, GROUP)],
                result.at[pl.ds(0, 8), pl.ds((core_ref[0] ^ part) * HALF + first, GROUP)],
                sems.at[len(copies)],
            ))
            copies[-1].start()
    for copy in copies:
        copy.wait()


def late_kernel(which, levels, core_ref, m, r, _, result, rows, sems):
    copies = []

    def write(p, row, v):
        rows[p - 8, row] = v

    for first in range(0, HALF, GROUP):
        interpolate(levels, range(8, 16), first, lambda p, row: m[p - 4, row] if p < 10 else r[p - 10, row], write)
        copies.append(pltpu.make_async_copy(
            rows.at[:, pl.ds(first, GROUP)],
            result.at[pl.ds(8, 8), pl.ds((core_ref[0] ^ which) * HALF + first, GROUP)],
            sems.at[len(copies)],
        ))
        copies[-1].start()
    for copy in copies:
        copy.wait()


VMEM = pl.BlockSpec(memory_space=pltpu.VMEM)
ANY = pl.BlockSpec(memory_space=pl.ANY)
SMEM = pl.BlockSpec(memory_space=pltpu.SMEM)
F32 = jnp.float32


def shape(*dims):
    return jax.ShapeDtypeStruct(dims, F32)


def call(kernel, name, specs, out_specs, outs, scratch, cost_us, aliases={}, vmem=24):
    return pl.pallas_call(
        kernel,
        name=name,
        out_shape=outs,
        in_specs=specs,
        out_specs=out_specs,
        scratch_shapes=scratch,
        input_output_aliases=aliases,
        cost_estimate=pl.CostEstimate(flops=0, bytes_accessed=int(cost_us * 3.69e6), transcendentals=0),
        compiler_params=pltpu.CompilerParams(vmem_limit_bytes=vmem << 20),
    )


def on_device(grids, tiles, state_field, levels, sign_bits):
    u = state_field.reshape(16, ROWS, 8, 128)

    def flat(y, core, rest):
        return ((y // 2) * 2 + core) * tiles + (y % 2) * (tiles // 2) + rest

    every = [(y, c, r) for y in range(grids) for c in range(2) for r in range(tiles // 2)]
    to_core = [(flat(y, c, r), flat(y, 1 - c, r)) for y, c, r in every]
    to_far = [(flat(y, c, r), flat((y + 2) % 4, c, r)) for y, c, r in every]

    def send(x, pairs):
        return lax.ppermute(x, ("grid", "tile"), pairs)

    tail, head = u[12:] * (1.0 / SCALE), u[:4] * (1.0 / SCALE)
    up = [(i, (i + 1) % tiles) for i in range(tiles)]
    down = [((i + 1) % tiles, i) for i in range(tiles)]
    left, right = lax.ppermute(tail, "tile", up), lax.ppermute(head, "tile", down)

    core = (lax.axis_index("grid") & 1).astype(jnp.int32).reshape(1)

    def buffers(n):
        return [pltpu.VMEM((n, ROWS, 8, 128), F32)] * 6

    half, edge = shape(4, HALF, 8, 128), shape(6, ROWS, 8, 128)
    keep_a, send_a, keep_b, send_b, edge_l, edge_r = call(
        middle_kernel, "middle", [SMEM] * 3 + [VMEM], (VMEM,) * 6, (shape(6, HALF, 8, 128),) * 2 + (shape(2, HALF, 8, 128),) * 2 + (edge,) * 2, buffers(16), 6, vmem=16,
    )(levels, sign_bits, core, u)
    got_a, got_b = send(send_a, to_core), send(send_b, to_core)
    part_m, part_b = keep_a + got_a, keep_b + got_b
    part_m, edge_l, edge_r = lax.optimization_barrier((part_m, edge_l, edge_r))
    far_m = send(part_m, to_far)
    keep_l, send_l, keep_r, send_r = call(
        outer_kernel, "outer", [SMEM] * 3 + [VMEM] * 5, (VMEM,) * 4, (half,) * 4, buffers(19), 6, vmem=20,
    )(levels, sign_bits, core, u, left, right, edge_l, edge_r)
    part_l = keep_l + send(send_l, to_core)
    part_r = jnp.concatenate([part_b, keep_r + send(send_r, to_core)])
    far_l = send(part_l, to_far)
    part_r, far_m = lax.optimization_barrier((part_r, far_m))
    far_r = send(part_r, to_far)
    own_l = part_l + far_l
    following = lax.ppermute(own_l[:1], "tile", down)
    other_l = send(own_l, to_core)
    own_m = part_m + far_m
    other_m = send(own_m, to_core)
    whole = shape(16, ROWS, 8, 128)
    result = call(
        early_kernel, "early", [SMEM] * 2 + [VMEM] * 4, ANY, whole,
        [pltpu.VMEM((2, 8, HALF, 8, 128), F32), pltpu.SemaphoreType.DMA((2 * HALF // GROUP,))], 1.5, vmem=8,
    )(levels, core, own_l, own_m, other_l, other_m)
    far_r, following, result = lax.optimization_barrier((far_r, following, result))
    own_r = jnp.concatenate([part_r + far_r, following])
    other_r = send(own_r, to_core)
    for which, m, r in ((0, own_m, own_r), (1, other_m, other_r)):
        result = call(
            functools.partial(late_kernel, which), ("late_own", "late_other")[which], [SMEM] * 2 + [VMEM] * 2 + [ANY],
            ANY, whole, [pltpu.VMEM((8, HALF, 8, 128), F32), pltpu.SemaphoreType.DMA((HALF // GROUP,))], 1, {4: 0}, vmem=8,
        )(levels, core, m, r, result)
    return result.reshape(state_field.shape)


def solution(mesh):
    grids, tiles = devices_of(mesh)
    placed = (P("grid", "tile", None, None, None, None, None), P("grid", None), P("grid"))
    return jax.shard_map(
        lambda *args: on_device(grids, tiles, *args),
        mesh=mesh,
        in_specs=placed,
        out_specs=P("grid", "tile", None, None, None, None, None),
        check_vma=False,
    )
```

```python
import functools

import jax
import jax.numpy as jnp
from jax import lax
from jax.experimental import pallas as pl
from jax.experimental.pallas import tpu as pltpu
from jax.sharding import PartitionSpec as P

SCALE = 6.4
ROWS = 32
HALF = ROWS // 2


def devices_of(mesh):
    return mesh.shape["grid"], mesh.shape["tile"]


def layer_update(src, layer, coef, masks, own, other, emit):
    vs, fs, gs = src
    low, ahead, behind = masks
    centre, rate = coef
    for d2 in range(2):
        base = own + d2 * 8
        above = own + 8 if d2 == 0 else other
        below = other + 8 if d2 == 0 else own
        f = [fs[layer, base + k] for k in range(8)]
        g = [gs[layer, base + k] for k in range(8)]
        for k in range(8):
            total = centre * vs[layer, base + k]
            total += rate[0] * (fs[layer + 1, base + k] + gs[layer - 1, base + k])
            total += rate[1] * (fs[layer, above + k] + gs[layer, below + k])
            total += rate[2] * (f[(k + 2) % 8] + g[(k + 6) % 8])
            pair = k ^ 1
            total += rate[3] * jnp.where(
                low, pltpu.roll(f[k] + g[pair], 4, 0), pltpu.roll(f[pair] + g[k], 4, 0)
            )
            total += rate[4] * (
                jnp.take_along_axis(f[k], ahead, axis=0, mode="promise_in_bounds")
                + jnp.take_along_axis(g[k], behind, axis=0, mode="promise_in_bounds")
            )
            total += rate[5] * (pltpu.roll(f[k], 127, 1) + pltpu.roll(g[k], 1, 1))
            emit(d2 * 8 + k, base + k, total)


def lane_masks():
    sub = lax.broadcasted_iota(jnp.int32, (8, 128), 0)
    group = sub - sub % 4
    return sub < 4, group + (sub + 1) % 4, group + (sub + 3) % 4


def coefficients(levels):
    rate = [0.08 / 16.0 * jnp.left_shift(jnp.int32(1), levels[0, d]).astype(jnp.float32) for d in range(6)]
    total = rate[0] + rate[1] + rate[2] + rate[3] + rate[4] + rate[5]
    return 1.0 - 2.0 * total, rate


def put(dst, layer, row, v):
    vs, fs, gs = dst
    q = v * v
    vs[layer, row] = v
    fs[layer, row] = v - q
    gs[layer, row] = v + q


def load_layer(dst, layer, source, index, scale):
    for row in range(ROWS):
        v = source[index, row]
        put(dst, layer, row, v * scale if scale is not None else v)


def step_layer(src, dst, layer, coef, masks):
    for half in range(2):
        layer_update(
            src, layer, coef, masks, half * HALF, (1 - half) * HALF,
            lambda at, row, v: put(dst, layer, row, v),
        )


def last_layer(src, layer, coef, masks, core, sign, keep, send, out):
    for part, ref in ((0, keep), (1, send)):
        own = (core ^ part) * HALF

        def emit(at, row, v, ref=ref):
            ref[out, at] = v * sign

        layer_update(src, layer, coef, masks, own, HALF - own, emit)


def loop(low, high, body, width=4):
    def several(i, carry):
        for j in range(width):
            body(low + width * i + j)
        return carry

    lax.fori_loop(0, (high - low) // width, several, 0)
    for i in range(high - (high - low) % width, high):
        body(i)


def middle_kernel(levels, signs, core_ref, u, keep_a, send_a, keep_b, send_b, edge_l, edge_r, *scratch):
    bufs = scratch[:3], scratch[3:]
    coef, masks = coefficients(levels), lane_masks()
    loop(0, 16, lambda i: load_layer(bufs[0], i, u, i, 1.0 / SCALE))
    for step in range(1, 4):
        src, dst = bufs[(step - 1) % 2], bufs[step % 2]
        loop(step, 16 - step, lambda i, s=src, d=dst: step_layer(s, d, i, coef, masks))
        for k in range(2):
            edge_l[2 * (step - 1) + k] = dst[0][step + k]
            edge_r[2 * (step - 1) + k] = dst[0][14 - step + k]
    core, sign = core_ref[0], (signs[0] * 2 - 1).astype(jnp.float32) * SCALE
    loop(0, 6, lambda i: last_layer(bufs[1], i + 4, coef, masks, core, sign, keep_a, send_a, i))
    loop(0, 2, lambda i: last_layer(bufs[1], i + 10, coef, masks, core, sign, keep_b, send_b, i))


def outer_kernel(levels, signs, core_ref, u, left, right, edge_l, edge_r, keep_l, send_l, keep_r, send_r, *scratch):
    bufs = scratch[:3], scratch[3:]
    coef, masks = coefficients(levels), lane_masks()
    for at, source, first, count, scale in (
        (0, left, 0, 4, None), (4, u, 0, 2, 1.0 / SCALE), (13, u, 14, 2, 1.0 / SCALE), (15, right, 0, 4, None)
    ):
        loop(
            0, count,
            lambda i, at=at, source=source, first=first, scale=scale: load_layer(bufs[0], at + i, source, first + i, scale),
        )
    for step in range(1, 4):
        src, dst = bufs[(step - 1) % 2], bufs[step % 2]
        for i in range(4):
            step_layer(src, dst, step + i, coef, masks)
            step_layer(src, dst, 15 - step + i, coef, masks)
        for k in range(2):
            load_layer(dst, 4 + step + k, edge_l, 2 * (step - 1) + k, None)
            load_layer(dst, 13 - step + k, edge_r, 2 * (step - 1) + k, None)
    core, sign = core_ref[0], (signs[0] * 2 - 1).astype(jnp.float32) * SCALE
    for i in range(4):
        last_layer(bufs[1], i + 4, coef, masks, core, sign, keep_l, send_l, i)
        last_layer(bufs[1], i + 11, coef, masks, core, sign, keep_r, send_r, i)


def interpolate(levels, points, first, read, write):
    for level in range(1, 5):

        @pl.when(levels[0, 0] == level)
        def _(space=1 << (4 - level)):
            for row in range(first, first + GROUP):
                kept = {}

                def keep(p, row=row, kept=kept):
                    if p not in kept:
                        kept[p] = read(p, row)
                    return kept[p]

                for p in points:
                    anchor, share = p // space * space, p % space / space
                    v = keep(anchor)
                    if share:
                        v = v * (1.0 - share) + keep(anchor + space) * share
                    write(p, row, v)


GROUP = 8


def early_kernel(levels, core_ref, own_l, own_m, other_l, other_m, result, rows, sems):
    copies = []
    for part, (l, m) in enumerate(((own_l, own_m), (other_l, other_m))):
        for first in range(0, HALF, GROUP):

            def write(p, row, v, part=part):
                rows[part, p, row] = v

            interpolate(levels, range(8), first, lambda p, row, l=l, m=m: l[p, row] if p < 4 else m[p - 4, row], write)
            copies.append(pltpu.make_async_copy(
                rows.at[part, :, pl.ds(first, GROUP)],
                result.at[pl.ds(0, 8), pl.ds((core_ref[0] ^ part) * HALF + first, GROUP)],
                sems.at[len(copies)],
            ))
            copies[-1].start()
    for copy in copies:
        copy.wait()


def late_kernel(which, levels, core_ref, m, r, _, result, rows, sems):
    copies = []

    def write(p, row, v):
        rows[p - 8, row] = v

    for first in range(0, HALF, GROUP):
        interpolate(levels, range(8, 16), first, lambda p, row: m[p - 4, row] if p < 10 else r[p - 10, row], write)
        copies.append(pltpu.make_async_copy(
            rows.at[:, pl.ds(first, GROUP)],
            result.at[pl.ds(8, 8), pl.ds((core_ref[0] ^ which) * HALF + first, GROUP)],
            sems.at[len(copies)],
        ))
        copies[-1].start()
    for copy in copies:
        copy.wait()


VMEM = pl.BlockSpec(memory_space=pltpu.VMEM)
ANY = pl.BlockSpec(memory_space=pl.ANY)
SMEM = pl.BlockSpec(memory_space=pltpu.SMEM)
F32 = jnp.float32


def shape(*dims):
    return jax.ShapeDtypeStruct(dims, F32)


def call(kernel, name, specs, out_specs, outs, scratch, cost_us, aliases={}, vmem=24):
    return pl.pallas_call(
        kernel,
        name=name,
        out_shape=outs,
        in_specs=specs,
        out_specs=out_specs,
        scratch_shapes=scratch,
        input_output_aliases=aliases,
        cost_estimate=pl.CostEstimate(flops=0, bytes_accessed=int(cost_us * 3.69e6), transcendentals=0),
        compiler_params=pltpu.CompilerParams(vmem_limit_bytes=vmem << 20),
    )


def on_device(grids, tiles, state_field, levels, sign_bits):
    u = state_field.reshape(16, ROWS, 8, 128)

    def flat(y, core, rest):
        return ((y // 2) * 2 + core) * tiles + (y % 2) * (tiles // 2) + rest

    every = [(y, c, r) for y in range(grids) for c in range(2) for r in range(tiles // 2)]
    to_core = [(flat(y, c, r), flat(y, 1 - c, r)) for y, c, r in every]
    to_far = [(flat(y, c, r), flat((y + 2) % 4, c, r)) for y, c, r in every]

    def send(x, pairs):
        return lax.ppermute(x, ("grid", "tile"), pairs)

    tail, head = u[12:] * (1.0 / SCALE), u[:4] * (1.0 / SCALE)
    up = [(i, (i + 1) % tiles) for i in range(tiles)]
    down = [((i + 1) % tiles, i) for i in range(tiles)]
    left, right = lax.ppermute(tail, "tile", up), lax.ppermute(head, "tile", down)

    core = (lax.axis_index("grid") & 1).astype(jnp.int32).reshape(1)

    def buffers(n):
        return [pltpu.VMEM((n, ROWS, 8, 128), F32)] * 6

    half, edge = shape(4, HALF, 8, 128), shape(6, ROWS, 8, 128)
    keep_a, send_a, keep_b, send_b, edge_l, edge_r = call(
        middle_kernel, "middle", [SMEM] * 3 + [VMEM], (VMEM,) * 6, (shape(6, HALF, 8, 128),) * 2 + (shape(2, HALF, 8, 128),) * 2 + (edge,) * 2, buffers(16), 6, vmem=16,
    )(levels, sign_bits, core, u)
    got_a, got_b = send(send_a, to_core), send(send_b, to_core)
    part_m, part_b = keep_a + got_a, keep_b + got_b
    part_m, edge_l, edge_r = lax.optimization_barrier((part_m, edge_l, edge_r))
    far_m = send(part_m, to_far)
    keep_l, send_l, keep_r, send_r = call(
        outer_kernel, "outer", [SMEM] * 3 + [VMEM] * 5, (VMEM,) * 4, (half,) * 4, buffers(19), 6, vmem=20,
    )(levels, sign_bits, core, u, left, right, edge_l, edge_r)
    part_l = keep_l + send(send_l, to_core)
    part_r = jnp.concatenate([part_b, keep_r + send(send_r, to_core)])
    far_l = send(part_l, to_far)
    part_r, far_m = lax.optimization_barrier((part_r, far_m))
    far_r = send(part_r, to_far)
    own_l = part_l + far_l
    following = lax.ppermute(own_l[:1], "tile", down)
    other_l = send(own_l, to_core)
    own_m = part_m + far_m
    other_m = send(own_m, to_core)
    whole = shape(16, ROWS, 8, 128)
    result = call(
        early_kernel, "early", [SMEM] * 2 + [VMEM] * 4, ANY, whole,
        [pltpu.VMEM((2, 8, HALF, 8, 128), F32), pltpu.SemaphoreType.DMA((2 * HALF // GROUP,))], 1.5, vmem=8,
    )(levels, core, own_l, own_m, other_l, other_m)
    far_r, following, result = lax.optimization_barrier((far_r, following, result))
    own_r = jnp.concatenate([part_r + far_r, following])
    other_r = send(own_r, to_core)
    for which, m, r in ((0, own_m, own_r), (1, other_m, other_r)):
        result = call(
            functools.partial(late_kernel, which), ("late_own", "late_other")[which], [SMEM] * 2 + [VMEM] * 2 + [ANY],
            ANY, whole, [pltpu.VMEM((8, HALF, 8, 128), F32), pltpu.SemaphoreType.DMA((HALF // GROUP,))], 1, {4: 0}, vmem=8,
        )(levels, core, m, r, result)
    return result.reshape(state_field.shape)


def solution(mesh):
    grids, tiles = devices_of(mesh)
    placed = (P("grid", "tile", None, None, None, None, None), P("grid", None), P("grid"))
    return jax.shard_map(
        lambda *args: on_device(grids, tiles, *args),
        mesh=mesh,
        in_specs=placed,
        out_specs=P("grid", "tile", None, None, None, None, None),
        check_vma=False,
    )
```
